512 devices in a mesh: seq: 64 (over y, z), tp: 8 (over x, core).
Axes of the slice: x: 4, y: 8, z: 8, core: 2. Of those that a mesh axis runs over, the one named last changes fastest.
Arguments:
- queries: bfloat16 [49152, 4096], P('seq', 'tp'), may hold values from -6 to 6
- key_rows: bfloat16 [49152, 4096], P('seq', 'tp'), may hold values from -6 to 6
- value_rows: bfloat16 [49152, 4096], P('seq', 'tp'), may hold values from -120 to 120
- log_decay: float32 [32, 49152], P('tp', 'seq'), may hold values from -10 to 0, as said below
- gate_logits: bfloat16 [49152, 4096], P('seq', 'tp'), may hold values from -6 to 6
- norm_gain: float32 [4096], P('tp'), may hold values from 0.1 to 1.9
- out_weight: bfloat16 [4096, 3072], P('tp'), may hold values from -0.125 to 0.125
Outputs:
- projected: bfloat16 [49152, 3072], P('seq', 'tp')
The draws below stay inside these ranges and needn't reach their ends.
Inputs may be any that keep to these rules, and one draw needn't show every extreme that they name: log_decay is never positive.
All inputs are finite; a program needn't handle non-finite values.
Results may differ from the reference program's by a relative error of at most 0.014.
Values may be sent and summed in bfloat16 or wider, within the bound.
A program may use at most 128 MiB of HBM per device.

```python
import math
import jax
import jax.numpy as jnp
from jax import lax

HEAD = 128
HEADS = 32
D_OUT = 3072
BLOCK = 384
T_DEV = 768
SEQUENCE_TOKENS = 49152
N_TP = 8


def draw_log_decay(key, part):
    key_matrix = jax.random.split(key, 7)
    fast_share = 0.5
    fast = jax.random.uniform(key_matrix[0], (HEADS, 1), jnp.float32) < fast_share
    fast_rate = jnp.exp(jax.random.uniform(key_matrix[1], (HEADS, 1), jnp.float32, math.log(10.0), math.log(17.0))) / BLOCK
    slow_rate = jnp.exp(jax.random.uniform(key_matrix[2], (HEADS, 1), jnp.float32, math.log(0.02), math.log(0.3))) / SEQUENCE_TOKENS
    baseline_decay_rate = jnp.where(fast, fast_rate, slow_rate)
    device_multiplier = jnp.exp(jax.random.uniform(key_matrix[3], (HEADS, SEQUENCE_TOKENS // T_DEV), jnp.float32, -math.log(2.0), math.log(2.0)))
    device_multiplier = jnp.repeat(device_multiplier, T_DEV, axis=1)
    token_multiplier = jnp.exp(jax.random.uniform(key_matrix[4], (HEADS, SEQUENCE_TOKENS), jnp.float32, -math.log(2.0), math.log(2.0)))
    sudden_spike = jax.random.uniform(key_matrix[5], (1, SEQUENCE_TOKENS), jnp.float32) < 3.0 / SEQUENCE_TOKENS
    feature_depth = jax.random.uniform(key_matrix[6], (HEADS, SEQUENCE_TOKENS), jnp.float32, math.log(0.5), math.log(0.8))
    value_matrix = -baseline_decay_rate * device_multiplier * token_multiplier + jnp.where(sudden_spike, feature_depth, 0.0)
    return value_matrix.astype(jnp.float32)


def draw_value_rows(key, part):
    key_matrix = jax.random.split(key, 3)
    columns = HEADS * HEAD
    row_scale = jnp.exp(jax.random.uniform(key_matrix[0], (SEQUENCE_TOKENS, 1), jnp.float32) * math.log(10.0))
    trend = jnp.exp(math.log(3.0) * (jnp.arange(columns) // HEAD).astype(jnp.float32) / max(HEADS - 1, 1))
    column_scale = jnp.exp(jax.random.uniform(key_matrix[1], (1, columns), jnp.float32) * math.log(10.0)) * trend[None, :]
    base = jnp.clip(jax.random.normal(key_matrix[2], (SEQUENCE_TOKENS, columns), jnp.float32), -4.0, 4.0)
    return (base * row_scale * column_scale / 10.0).astype(jnp.bfloat16)


def strengthened(drawn, stream_key, source, target, blocks, factor):
    owner, partner = [(jnp.arange(drawn.shape[position]) // (drawn.shape[position] // blocks)).reshape([-1 if axis == position else 1 for axis in range(drawn.ndim)]) for position in (source, target)]
    chosen = jax.random.permutation(stream_key, blocks)[partner]
    strong = (owner == chosen) | (owner == (partner + blocks // 2) % blocks)
    return jnp.where(strong, factor * drawn, drawn)


def steps_of(key, dims, shards, smallest, high):
    loudness = 1.0
    for position, parts in shards:
        draws = jax.random.uniform(jax.random.fold_in(jax.random.fold_in(key, 6), position), (parts,), jnp.float32, smallest / len(shards), high / len(shards))
        loudness = loudness * jnp.repeat(jnp.exp(draws), dims[position] // parts).reshape((-1,) + (1,) * (len(dims) - 1 - position))
    return loudness


def scatter_about(stream_key, extent, width, limit, pieces=(), kind=jnp.bfloat16):
    level = steps_of(stream_key, extent, pieces, -0.22, 0.18) if pieces else 1.0
    drawn = jax.random.normal(stream_key, extent, jnp.float32) * width * level
    return jnp.minimum(jnp.maximum(drawn, -limit), limit).astype(kind)


def noise_with(stream_key, shape, scale, limit, shards, heavy, held_as=jnp.bfloat16):
    result = scale * jax.random.normal(stream_key, shape, jnp.float32)
    if shards:
        result = result * steps_of(stream_key, shape, shards, -0.22, 0.18)
    return jnp.clip(strengthened(result, jax.random.fold_in(stream_key, 3), *heavy), -limit, limit).astype(held_as)


def setup_inputs(seed: int = 0) -> dict:
    key_of = jax.random.split(jax.random.key(seed), 8)
    return {
        "queries": scatter_about(key_of[0], (SEQUENCE_TOKENS, HEADS * HEAD), 1.0, 6.0, ((0, 64), (1, 8))),
        "key_rows": scatter_about(key_of[1], (SEQUENCE_TOKENS, HEADS * HEAD), 1.0, 6.0, ((0, 64), (1, 8))),
        "value_rows": draw_value_rows(jax.random.fold_in(key_of[7], 71), 0),
        "log_decay": draw_log_decay(jax.random.fold_in(key_of[7], 71), 0),
        "gate_logits": scatter_about(key_of[4], (SEQUENCE_TOKENS, HEADS * HEAD), 1.5, 6.0, ((0, 64), (1, 8))),
        "norm_gain": jnp.clip(1.0 + 0.18 * jax.random.normal(key_of[5], (HEADS * HEAD,), jnp.float32), 0.1, 1.9),
        "out_weight": noise_with(key_of[6], (HEADS * HEAD, D_OUT), (HEADS * HEAD) ** -0.5, 0.125, ((0, 8),), (0, 1, 8, 2.0)),
    }


def reference(queries, key_rows, value_rows, log_decay, gate_logits, norm_gain, out_weight):
    blocks = SEQUENCE_TOKENS // BLOCK
    columns = HEADS * HEAD
    query_blocks = queries.reshape(blocks, BLOCK, HEADS, HEAD)
    key_blocks = key_rows.reshape(blocks, BLOCK, HEADS, HEAD)
    value_blocks = value_rows.reshape(blocks, BLOCK, HEADS, HEAD)
    decays = log_decay.reshape(HEADS, blocks, BLOCK).transpose(1, 0, 2)
    causal = jnp.tril(jnp.ones((BLOCK, BLOCK), dtype=jnp.bool_))

    def advance(states, inputs):
        query_here, key_here, value_here, decay_here = inputs
        cumulative = jnp.cumsum(decay_here, axis=1)
        totals = cumulative[:, -1]
        spread = cumulative[:, :, None] - cumulative[:, None, :]
        weights = jnp.where(causal, jnp.exp(jnp.where(causal, spread, 0.0)), 0.0)
        scores = jnp.einsum('tha,sha->hts', query_here.astype(jnp.float32), key_here.astype(jnp.float32))
        weighted = (scores * weights).astype(jnp.bfloat16)
        inside = jnp.einsum('hts,shb->thb', weighted.astype(jnp.float32), value_here.astype(jnp.float32))
        scaled_queries = query_here.astype(jnp.float32) * jnp.exp(cumulative).T[:, :, None]
        carried = jnp.einsum('tha,hab->thb', scaled_queries, states, precision=lax.Precision.HIGHEST)
        scaled_keys = (key_here.astype(jnp.float32) * jnp.exp(totals[:, None] - cumulative).T[:, :, None]).astype(jnp.bfloat16)
        block_state = jnp.einsum('tha,thb->hab', scaled_keys.astype(jnp.float32), value_here.astype(jnp.float32))
        updated = jnp.exp(totals)[:, None, None] * states + block_state
        return (updated, inside + carried)
    initial = jnp.zeros((HEADS, HEAD, HEAD), jnp.float32)
    _, attention = lax.scan(advance, initial, (query_blocks, key_blocks, value_blocks, decays))
    attention = attention.reshape(SEQUENCE_TOKENS, columns)
    mean_square = lax.optimization_barrier(jnp.mean(attention * attention, axis=1))
    gates = jax.nn.sigmoid(gate_logits.astype(jnp.float32))
    attended = (attention * lax.rsqrt(mean_square + 1e-06)[:, None] * norm_gain * gates).astype(jnp.bfloat16)
    group_width = columns // N_TP
    summed = jnp.zeros((SEQUENCE_TOKENS, D_OUT), jnp.float32)
    for group in range(N_TP):
        lower = group * group_width
        partial_sum = jnp.dot(attended[:, lower:lower + group_width], out_weight[lower:lower + group_width], preferred_element_type=jnp.float32).astype(jnp.bfloat16)
        partial_sum = lax.optimization_barrier(partial_sum)
        summed = summed + partial_sum.astype(jnp.float32)
    return summed.astype(jnp.bfloat16)
```

```python
import jax
import jax.numpy as jnp
from jax import lax
from jax.sharding import PartitionSpec as P

HEAD = 128
HEADS = 32
BLOCK = 384


def exchange(running, decay_sum):
    head_count = running.shape[0]
    ways = lax.axis_size("seq")
    per_head = ways // head_count
    rows = HEAD // per_head
    pieces = running.astype(jnp.bfloat16).reshape(ways, rows, HEAD)
    high = lax.reduce_precision(decay_sum, 8, 7)
    middle = lax.reduce_precision(decay_sum - high, 8, 7)
    low = lax.reduce_precision(decay_sum - high - middle, 8, 7)
    parts = jnp.stack([high, middle, low] + [jnp.zeros_like(high)] * (rows - 3), axis=1)
    parts = jnp.repeat(parts.astype(jnp.bfloat16), per_head, axis=0)
    parts = jnp.broadcast_to(parts[:, :, None], (ways, rows, HEAD))
    sent = jnp.concatenate([pieces, parts], axis=1)
    got = lax.all_to_all(sent, "seq", 0, 0, tiled=True).astype(jnp.float32)
    states = got[:, :rows].reshape(ways, rows * HEAD)
    totals = jnp.sum(got[:, rows : rows + 3, 0], axis=1)
    place = jnp.arange(ways)
    target, origin, between = place[None, :, None], place[None, None, :], place[:, None, None]
    inside = (between > origin) & (between < target)
    spans = jnp.sum(jnp.where(inside, totals[:, None, None], 0.0), axis=0)
    factors = jnp.where(place[None, :] < place[:, None], jnp.exp(spans), 0.0)
    starts = jnp.dot(factors, states, precision=lax.Precision.HIGHEST)
    back = starts.astype(jnp.bfloat16).reshape(ways, rows, HEAD)
    mine = lax.all_to_all(back, "seq", 0, 0, tiled=True)
    return mine.astype(jnp.float32).reshape(head_count, HEAD, HEAD)


def shards(queries, key_rows, value_rows, log_decay, gate_logits, norm_gain, out_weight):
    rows_here = queries.shape[0]
    columns = queries.shape[1]
    head_count = columns // HEAD
    blocks = rows_here // BLOCK
    query_blocks = queries.reshape(blocks, BLOCK, head_count, HEAD)
    key_blocks = key_rows.reshape(blocks, BLOCK, head_count, HEAD)
    value_blocks = value_rows.reshape(blocks, BLOCK, head_count, HEAD)
    cumulative = jnp.cumsum(log_decay.reshape(head_count, blocks, BLOCK), axis=2)
    totals = cumulative[:, :, -1]
    causal = jnp.tril(jnp.ones((BLOCK, BLOCK), dtype=jnp.bool_))
    spread = cumulative[:, :, :, None] - cumulative[:, :, None, :]
    decays = jnp.where(causal, jnp.exp(jnp.where(causal, spread, 0.0)), 0.0)
    scores = jnp.einsum(
        "ntha,nsha->hnts", query_blocks, key_blocks, preferred_element_type=jnp.float32
    )
    weighted = (scores * decays).astype(jnp.bfloat16)
    inside = jnp.einsum(
        "hnts,nshb->nthb", weighted, value_blocks, preferred_element_type=jnp.float32
    )
    key_scale = jnp.exp(totals[:, :, None] - cumulative).transpose(1, 2, 0)[..., None]
    scaled_keys = (key_blocks.astype(jnp.float32) * key_scale).astype(jnp.bfloat16)
    block_states = jnp.einsum(
        "ntha,nthb->nhab", scaled_keys, value_blocks, preferred_element_type=jnp.float32
    )
    running = jnp.zeros((head_count, HEAD, HEAD), jnp.float32)
    decay_sum = jnp.zeros((head_count,), jnp.float32)
    local_before = []
    decay_before = []
    for block in range(blocks):
        local_before.append(running)
        decay_before.append(decay_sum)
        running = jnp.exp(totals[:, block])[:, None, None] * running + block_states[block]
        decay_sum = decay_sum + totals[:, block]
    incoming = exchange(running, decay_sum)
    starts = jnp.stack(
        [
            jnp.exp(decay_before[block])[:, None, None] * incoming + local_before[block]
            for block in range(blocks)
        ]
    )
    query_scale = jnp.exp(cumulative).transpose(1, 2, 0)[..., None]
    scaled_queries = query_blocks.astype(jnp.float32) * query_scale
    carried = jnp.einsum("ntha,nhab->nthb", scaled_queries, starts, precision=lax.Precision.HIGHEST)
    attention = (inside + carried).reshape(rows_here, columns)
    squares = jnp.sum(attention * attention, axis=1)
    gates = jax.nn.sigmoid(gate_logits.astype(jnp.float32))
    attended = (attention * norm_gain * gates).astype(jnp.bfloat16)
    ways = lax.axis_size("tp")
    product = lax.dot_general(
        out_weight, attended, (((0,), (1,)), ((), ())), preferred_element_type=jnp.float32
    ).astype(jnp.bfloat16)
    width = product.shape[0] // ways
    extra = jnp.broadcast_to(squares.astype(jnp.bfloat16), (ways, 16, rows_here))
    sent = jnp.concatenate([product.reshape(ways, width, rows_here), extra], axis=1)
    summed = lax.psum_scatter(
        sent.reshape(ways * (width + 16), rows_here), "tp", scatter_dimension=0, tiled=True
    ).astype(jnp.float32)
    mean_square = summed[width] / (HEADS * HEAD)
    return (summed[:width] * lax.rsqrt(mean_square + 1e-06)).T.astype(jnp.bfloat16)


def solution(mesh):
    return jax.shard_map(
        shards,
        mesh=mesh,
        in_specs=(
            P("seq", "tp"),
            P("seq", "tp"),
            P("seq", "tp"),
            P("tp", "seq"),
            P("seq", "tp"),
            P("tp"),
            P("tp", None),
        ),
        out_specs=P("seq", "tp"),
        check_vma=False,
    )
```

```python
import jax
import jax.numpy as jnp
from jax import lax
from jax.experimental import pallas as pl
from jax.experimental.pallas import tpu as pltpu
from jax.sharding import PartitionSpec as P

HEAD = 128
HEADS = 32
BLOCK = 384


def exchange(running, decay_sum):
    head_count = running.shape[0]
    ways = lax.axis_size("seq")
    per_head = ways // head_count
    rows = HEAD // per_head
    pieces = running.astype(jnp.bfloat16).reshape(ways, rows, HEAD)
    high = lax.reduce_precision(decay_sum, 8, 7)
    middle = lax.reduce_precision(decay_sum - high, 8, 7)
    low = lax.reduce_precision(decay_sum - high - middle, 8, 7)
    parts = jnp.stack([high, middle, low] + [jnp.zeros_like(high)] * (rows - 3), axis=1)
    parts = jnp.repeat(parts.astype(jnp.bfloat16), per_head, axis=0)
    parts = jnp.broadcast_to(parts[:, :, None], (ways, rows, HEAD))
    sent = jnp.concatenate([pieces, parts], axis=1)
    got = lax.all_to_all(sent, "seq", 0, 0, tiled=True).astype(jnp.float32)
    states = got[:, :rows].reshape(ways, rows * HEAD)
    totals = jnp.sum(got[:, rows : rows + 3, 0], axis=1)
    place = jnp.arange(ways)
    target, origin, between = place[None, :, None], place[None, None, :], place[:, None, None]
    inside = (between > origin) & (between < target)
    spans = jnp.sum(jnp.where(inside, totals[:, None, None], 0.0), axis=0)
    factors = jnp.where(place[None, :] < place[:, None], jnp.exp(spans), 0.0)
    starts = jnp.dot(factors, states, precision=lax.Precision.HIGHEST)
    back = starts.astype(jnp.bfloat16).reshape(ways, rows, HEAD)
    mine = lax.all_to_all(back, "seq", 0, 0, tiled=True)
    return mine.astype(jnp.float32).reshape(head_count, HEAD, HEAD)


def project_kernel(
    a_ref, w_ref, sq_ref, o_ref,
    give, got, held, own, relay, landed, squares,
    give_send, give_recv, far_send, far_recv, near_send, near_recv,
    last_send, last_recv, sq_send, sq_recv,
):
    tokens, width = o_ref.shape
    half = tokens // 2
    tile = tokens // 3
    me = lax.axis_index("tp")
    core = lax.rem(me, 2)
    chip = lax.div(me, 2)

    def device(step, which):
        return lax.rem(chip + step, 4) * 2 + which

    sibling = device(0, 1 - core)
    right, left = device(1, core), device(3, core)

    barrier = pltpu.get_barrier_semaphore()
    for offset in range(1, 8):
        pl.semaphore_signal(
            barrier, inc=1, device_id={"tp": lax.rem(me + offset, 8)},
            device_id_type=pl.DeviceIdType.MESH,
        )
    pl.semaphore_wait(barrier, 7)

    def send(source, target, send_sem, recv_sem, to):
        copy = pltpu.make_async_remote_copy(
            src_ref=source, dst_ref=target, send_sem=send_sem, recv_sem=recv_sem,
            device_id={"tp": to}, device_id_type=pl.DeviceIdType.MESH,
        )
        copy.start()
        return copy

    copies = []
    sq_copies = [
        send(sq_ref, squares.at[i], sq_send.at[i], sq_recv.at[i], lax.rem(me + i + 1, 8))
        for i in range(7)
    ]

    def tiles(body):
        def step(i, carry):
            body(pl.ds(pl.multiple_of(i * tile, tile), tile))
            return carry

        lax.fori_loop(0, 3, step, 0)

    def product(dest, rows):
        columns = pl.ds(pl.multiple_of(dest * width, 128), width)
        return jnp.dot(a_ref[rows, :], w_ref[:, columns], preferred_element_type=jnp.float32)

    steps = (2, 1, 3, 0)
    gives = []

    def hand_over(k):
        def body(rows):
            give[k, rows, :] = product(device(steps[k], 1 - core), rows).astype(jnp.bfloat16)

        tiles(body)
        gives.append(send(give.at[k], got.at[k], give_send.at[k], give_recv.at[k], sibling))

    def gather(k, target, dtype):
        def first(rows):
            own[rows, :] = product(device(steps[k], core), rows)

        tiles(first)
        gives[k].wait_recv()

        def second(rows):
            total = own[rows, :] + got[k, rows, :].astype(jnp.float32)
            if dtype is None:
                own[rows, :] = total
            else:
                target[k, rows, :] = total.astype(dtype)

        tiles(second)

    top, bottom = pl.ds(0, half), pl.ds(half, half)
    hand_over(0)
    hand_over(1)
    gather(0, held, jnp.bfloat16)
    far_right = send(held.at[0, top], relay.at[0], far_send.at[0], far_recv.at[0], right)
    far_left = send(held.at[0, bottom], relay.at[1], far_send.at[1], far_recv.at[1], left)
    hand_over(2)
    gather(1, held, jnp.bfloat16)
    near_right = send(
        held.at[1, bottom], landed.at[0, bottom], near_send.at[0], near_recv.at[0], right
    )
    hand_over(3)
    gather(2, held, jnp.bfloat16)
    near_left = send(held.at[2, top], landed.at[1, top], near_send.at[1], near_recv.at[1], left)
    gather(3, None, None)

    def merge(k, start, slot):
        piece = half // 3

        def step(i, carry):
            rows = pl.ds(pl.multiple_of(start + i * piece, piece), piece)
            here = pl.ds(pl.multiple_of(i * piece, piece), piece)
            total = held[k, rows, :].astype(jnp.float32) + relay[slot, here, :].astype(jnp.float32)
            held[k, rows, :] = total.astype(jnp.bfloat16)
            return carry

        lax.fori_loop(0, 3, step, 0)

    far_right.wait_recv()
    merge(1, 0, 0)
    last_right = send(held.at[1, top], landed.at[0, top], last_send.at[0], last_recv.at[0], right)
    far_left.wait_recv()
    merge(2, half, 1)
    last_left = send(
        held.at[2, bottom], landed.at[1, bottom], last_send.at[1], last_recv.at[1], left
    )
    total = sq_ref[...]
    for i in range(7):
        sq_copies[i].wait_recv()
        total = total + squares[i]
    scale = lax.rsqrt(total / (HEADS * HEAD) + 1e-06)
    scale = jnp.transpose(jnp.broadcast_to(scale, (8, tokens)))[:, :1]
    near_right.wait_recv()
    near_left.wait_recv()
    last_right.wait_recv()
    last_left.wait_recv()
    for i in range(3):
        rows = slice(i * tile, (i + 1) * tile)
        summed = (
            own[rows, :]
            + landed[0, rows, :].astype(jnp.float32)
            + landed[1, rows, :].astype(jnp.float32)
        )
        o_ref[rows, :] = (summed * scale[rows]).astype(o_ref.dtype)
    for copy in sq_copies + gives + [
        far_right, far_left, near_right, near_left, last_right, last_left
    ]:
        copy.wait_send()


def project(attended, out_weight, squares):
    tokens = attended.shape[0]
    width = out_weight.shape[1] // 8
    block = (4, tokens, width)
    pair = pltpu.SemaphoreType.DMA((2,))
    four = pltpu.SemaphoreType.DMA((4,))
    seven = pltpu.SemaphoreType.DMA((7,))
    vmem = pl.BlockSpec(memory_space=pltpu.VMEM)
    return pl.pallas_call(
        project_kernel,
        out_shape=jax.ShapeDtypeStruct((tokens, width), jnp.bfloat16),
        in_specs=[vmem] * 3,
        out_specs=vmem,
        scratch_shapes=[
            pltpu.VMEM(block, jnp.bfloat16),
            pltpu.VMEM(block, jnp.bfloat16),
            pltpu.VMEM((3, tokens, width), jnp.bfloat16),
            pltpu.VMEM((tokens, width), jnp.float32),
            pltpu.VMEM((2, tokens // 2, width), jnp.bfloat16),
            pltpu.VMEM((2, tokens, width), jnp.bfloat16),
            pltpu.VMEM((7, 1, tokens), jnp.float32),
            four, four, pair, pair, pair, pair, pair, pair, seven, seven,
        ],
        compiler_params=pltpu.CompilerParams(
            collective_id=0, has_side_effects=True, vmem_limit_bytes=40 << 20
        ),
    )(attended, out_weight, squares)


def shards(queries, key_rows, value_rows, log_decay, gate_logits, norm_gain, out_weight):
    rows_here = queries.shape[0]
    columns = queries.shape[1]
    head_count = columns // HEAD
    blocks = rows_here // BLOCK
    query_blocks = queries.reshape(blocks, BLOCK, head_count, HEAD)
    key_blocks = key_rows.reshape(blocks, BLOCK, head_count, HEAD)
    value_blocks = value_rows.reshape(blocks, BLOCK, head_count, HEAD)
    cumulative = jnp.cumsum(log_decay.reshape(head_count, blocks, BLOCK), axis=2)
    totals = cumulative[:, :, -1]
    causal = jnp.tril(jnp.ones((BLOCK, BLOCK), dtype=jnp.bool_))
    spread = cumulative[:, :, :, None] - cumulative[:, :, None, :]
    decays = jnp.where(causal, jnp.exp(jnp.where(causal, spread, 0.0)), 0.0)
    scores = jnp.einsum(
        "ntha,nsha->hnts", query_blocks, key_blocks, preferred_element_type=jnp.float32
    )
    weighted = (scores * decays).astype(jnp.bfloat16)
    inside = jnp.einsum(
        "hnts,nshb->nthb", weighted, value_blocks, preferred_element_type=jnp.float32
    )
    key_scale = jnp.exp(totals[:, :, None] - cumulative).transpose(1, 2, 0)[..., None]
    scaled_keys = (key_blocks.astype(jnp.float32) * key_scale).astype(jnp.bfloat16)
    block_states = jnp.einsum(
        "ntha,nthb->nhab", scaled_keys, value_blocks, preferred_element_type=jnp.float32
    )
    running = jnp.zeros((head_count, HEAD, HEAD), jnp.float32)
    decay_sum = jnp.zeros((head_count,), jnp.float32)
    local_before = []
    decay_before = []
    for block in range(blocks):
        local_before.append(running)
        decay_before.append(decay_sum)
        running = jnp.exp(totals[:, block])[:, None, None] * running + block_states[block]
        decay_sum = decay_sum + totals[:, block]
    incoming = exchange(running, decay_sum)
    starts = jnp.stack(
        [
            jnp.exp(decay_before[block])[:, None, None] * incoming + local_before[block]
            for block in range(blocks)
        ]
    )
    query_scale = jnp.exp(cumulative).transpose(1, 2, 0)[..., None]
    scaled_queries = query_blocks.astype(jnp.float32) * query_scale
    carried = jnp.einsum("ntha,nhab->nthb", scaled_queries, starts, precision=lax.Precision.HIGHEST)
    attention = (inside + carried).reshape(rows_here, columns)
    squares = jnp.sum(attention * attention, axis=1)
    gates = jax.nn.sigmoid(gate_logits.astype(jnp.float32))
    attended = (attention * norm_gain * gates).astype(jnp.bfloat16)
    return project(attended, out_weight, squares[None, :])


def solution(mesh):
    return jax.shard_map(
        shards,
        mesh=mesh,
        in_specs=(
            P("seq", "tp"),
            P("seq", "tp"),
            P("seq", "tp"),
            P("tp", "seq"),
            P("seq", "tp"),
            P("tp"),
            P("tp", None),
        ),
        out_specs=P("seq", "tp"),
        check_vma=False,
    )
```

```python
import jax
import jax.numpy as jnp
from jax import lax
from jax.experimental import pallas as pl
from jax.experimental.pallas import tpu as pltpu
from jax.sharding import PartitionSpec as P

HEAD = 128
HEADS = 32
BLOCK = 384


def exchange_kernel(
    state_ref, total_ref, o_ref,
    states, totals, row_state, row_total, rows_got, row_totals_got, back, mine,
    state_send, state_recv, total_send, total_recv, row_send, row_recv,
    row_total_send, row_total_recv, back_send, back_recv,
):
    me = lax.axis_index("seq")
    near = lax.rem(me, 8)
    far = lax.div(me, 8)
    head = lax.div(near, 2)

    def along(offset):
        return far * 8 + lax.rem(near + offset, 8)

    def across(offset):
        return lax.rem(far + offset, 8) * 8 + near

    barrier = pltpu.get_barrier_semaphore()
    for offset in range(1, 8):
        for peer in (along(offset), across(offset)):
            pl.semaphore_signal(
                barrier, inc=1, device_id={"seq": peer}, device_id_type=pl.DeviceIdType.MESH
            )
    pl.semaphore_wait(barrier, 14)

    def send(source, target, send_sem, recv_sem, to):
        copy = pltpu.make_async_remote_copy(
            src_ref=source, dst_ref=target, send_sem=send_sem, recv_sem=recv_sem,
            device_id={"seq": to}, device_id_type=pl.DeviceIdType.MESH,
        )
        copy.start()
        return copy

    order = (4, 3, 5, 2, 6, 1, 7)
    first = []
    for offset in order:
        i = offset - 1
        peer = lax.rem(near + offset, 8)
        first.append(
            send(total_ref, totals.at[near], total_send.at[i], total_recv.at[i], along(offset))
        )
        first.append(
            send(
                state_ref.at[peer], states.at[near],
                state_send.at[i], state_recv.at[i], along(offset),
            )
        )
    totals[near] = total_ref[...]
    states[near] = state_ref[near]
    for copy in first:
        copy.wait_recv()
    decays = []
    pieces = []
    total = jnp.zeros(total_ref.shape, jnp.float32)
    running = jnp.zeros(o_ref.shape[1:], jnp.float32)
    for z in range(8):
        decay = jnp.exp(totals[z, pl.ds(head, 1), :])
        piece = states[z].astype(jnp.float32)
        running = decay * running + piece
        total = total + totals[z]
        decays.append(decay)
        pieces.append(piece)
    row_state[...] = running.astype(jnp.bfloat16)
    row_total[...] = total
    second = []
    for offset in order:
        i = offset - 1
        second.append(
            send(
                row_total, row_totals_got.at[far],
                row_total_send.at[i], row_total_recv.at[i], across(offset),
            )
        )
        second.append(
            send(row_state, rows_got.at[far], row_send.at[i], row_recv.at[i], across(offset))
        )
    rows_got[far] = row_state[...]
    row_totals_got[far] = row_total[...]
    for copy in second:
        copy.wait_recv()
    running = jnp.zeros(o_ref.shape[1:], jnp.float32)
    for y in range(8):
        decay = jnp.exp(row_totals_got[y, pl.ds(head, 1), :])
        moved = decay * running + rows_got[y].astype(jnp.float32)
        running = jnp.where(y < far, moved, running)
    for z in range(8):
        back[z] = running.astype(jnp.bfloat16)
        running = decays[z] * running + pieces[z]
    third = []
    for offset in order:
        i = offset - 1
        peer = lax.rem(near + offset, 8)
        third.append(
            send(back.at[peer], mine.at[near], back_send.at[i], back_recv.at[i], along(offset))
        )
    mine[near] = back[near]
    for copy in third:
        copy.wait_recv()
    o_ref[...] = mine[...].astype(jnp.float32)
    for copy in first + second + third:
        copy.wait_send()


def exchange(running, decay_sum):
    head_count = running.shape[0]
    rows = head_count * HEAD // 8
    pieces = running.astype(jnp.bfloat16).reshape(8, rows, HEAD)
    totals = jnp.pad(
        jnp.broadcast_to(decay_sum[:, None], (head_count, HEAD)), ((0, 8 - head_count), (0, 0))
    )
    seven = pltpu.SemaphoreType.DMA((7,))
    vmem = pl.BlockSpec(memory_space=pltpu.VMEM)
    block = pltpu.VMEM((8, rows, HEAD), jnp.bfloat16)
    sums = pltpu.VMEM((8, 8, HEAD), jnp.float32)
    incoming = pl.pallas_call(
        exchange_kernel,
        out_shape=jax.ShapeDtypeStruct((8, rows, HEAD), jnp.float32),
        in_specs=[vmem] * 2,
        out_specs=vmem,
        scratch_shapes=[
            block, sums,
            pltpu.VMEM((rows, HEAD), jnp.bfloat16),
            pltpu.VMEM((8, HEAD), jnp.float32),
            block, sums, block, block,
        ] + [seven] * 10,
        compiler_params=pltpu.CompilerParams(collective_id=1, has_side_effects=True),
    )(pieces, totals)
    return incoming.reshape(head_count, HEAD, HEAD)


def project_kernel(
    a_ref, w_ref, sq_ref, o_ref,
    give, got, held, own, relay, landed, squares,
    give_send, give_recv, far_send, far_recv, near_send, near_recv,
    last_send, last_recv, sq_send, sq_recv,
):
    tokens, width = o_ref.shape
    half = tokens // 2
    tile = tokens // 3
    me = lax.axis_index("tp")
    core = lax.rem(me, 2)
    chip = lax.div(me, 2)

    def device(step, which):
        return lax.rem(chip + step, 4) * 2 + which

    sibling = device(0, 1 - core)
    right, left = device(1, core), device(3, core)

    barrier = pltpu.get_barrier_semaphore()
    for offset in range(1, 8):
        pl.semaphore_signal(
            barrier, inc=1, device_id={"tp": lax.rem(me + offset, 8)},
            device_id_type=pl.DeviceIdType.MESH,
        )
    pl.semaphore_wait(barrier, 7)

    def send(source, target, send_sem, recv_sem, to):
        copy = pltpu.make_async_remote_copy(
            src_ref=source, dst_ref=target, send_sem=send_sem, recv_sem=recv_sem,
            device_id={"tp": to}, device_id_type=pl.DeviceIdType.MESH,
        )
        copy.start()
        return copy

    copies = []
    sq_copies = [
        send(sq_ref, squares.at[i], sq_send.at[i], sq_recv.at[i], lax.rem(me + i + 1, 8))
        for i in range(7)
    ]

    def tiles(body):
        def step(i, carry):
            body(pl.ds(pl.multiple_of(i * tile, tile), tile))
            return carry

        lax.fori_loop(0, 3, step, 0)

    def product(dest, rows):
        columns = pl.ds(pl.multiple_of(dest * width, 128), width)
        return jnp.dot(a_ref[rows, :], w_ref[:, columns], preferred_element_type=jnp.float32)

    steps = (2, 1, 3, 0)
    gives = []

    def hand_over(k):
        def body(rows):
            give[k, rows, :] = product(device(steps[k], 1 - core), rows).astype(jnp.bfloat16)

        tiles(body)
        gives.append(send(give.at[k], got.at[k], give_send.at[k], give_recv.at[k], sibling))

    def gather(k, target, dtype):
        def first(rows):
            own[rows, :] = product(device(steps[k], core), rows)

        tiles(first)
        gives[k].wait_recv()

        def second(rows):
            total = own[rows, :] + got[k, rows, :].astype(jnp.float32)
            if dtype is None:
                own[rows, :] = total
            else:
                target[k, rows, :] = total.astype(dtype)

        tiles(second)

    top, bottom = pl.ds(0, half), pl.ds(half, half)
    hand_over(0)
    hand_over(1)
    gather(0, held, jnp.bfloat16)
    far_right = send(held.at[0, top], relay.at[0], far_send.at[0], far_recv.at[0], right)
    far_left = send(held.at[0, bottom], relay.at[1], far_send.at[1], far_recv.at[1], left)
    hand_over(2)
    gather(1, held, jnp.bfloat16)
    near_right = send(
        held.at[1, bottom], landed.at[0, bottom], near_send.at[0], near_recv.at[0], right
    )
    hand_over(3)
    gather(2, held, jnp.bfloat16)
    near_left = send(held.at[2, top], landed.at[1, top], near_send.at[1], near_recv.at[1], left)
    gather(3, None, None)

    def merge(k, start, slot):
        piece = half // 3

        def step(i, carry):
            rows = pl.ds(pl.multiple_of(start + i * piece, piece), piece)
            here = pl.ds(pl.multiple_of(i * piece, piece), piece)
            total = held[k, rows, :].astype(jnp.float32) + relay[slot, here, :].astype(jnp.float32)
            held[k, rows, :] = total.astype(jnp.bfloat16)
            return carry

        lax.fori_loop(0, 3, step, 0)

    far_right.wait_recv()
    merge(1, 0, 0)
    last_right = send(held.at[1, top], landed.at[0, top], last_send.at[0], last_recv.at[0], right)
    far_left.wait_recv()
    merge(2, half, 1)
    last_left = send(
        held.at[2, bottom], landed.at[1, bottom], last_send.at[1], last_recv.at[1], left
    )
    total = sq_ref[...]
    for i in range(7):
        sq_copies[i].wait_recv()
        total = total + squares[i]
    scale = lax.rsqrt(total / (HEADS * HEAD) + 1e-06)
    scale = jnp.transpose(jnp.broadcast_to(scale, (8, tokens)))[:, :1]
    near_right.wait_recv()
    near_left.wait_recv()
    last_right.wait_recv()
    last_left.wait_recv()
    for i in range(3):
        rows = slice(i * tile, (i + 1) * tile)
        summed = (
            own[rows, :]
            + landed[0, rows, :].astype(jnp.float32)
            + landed[1, rows, :].astype(jnp.float32)
        )
        o_ref[rows, :] = (summed * scale[rows]).astype(o_ref.dtype)
    for copy in sq_copies + gives + [
        far_right, far_left, near_right, near_left, last_right, last_left
    ]:
        copy.wait_send()


def project(attended, out_weight, squares):
    tokens = attended.shape[0]
    width = out_weight.shape[1] // 8
    block = (4, tokens, width)
    pair = pltpu.SemaphoreType.DMA((2,))
    four = pltpu.SemaphoreType.DMA((4,))
    seven = pltpu.SemaphoreType.DMA((7,))
    vmem = pl.BlockSpec(memory_space=pltpu.VMEM)
    return pl.pallas_call(
        project_kernel,
        out_shape=jax.ShapeDtypeStruct((tokens, width), jnp.bfloat16),
        in_specs=[vmem] * 3,
        out_specs=vmem,
        scratch_shapes=[
            pltpu.VMEM(block, jnp.bfloat16),
            pltpu.VMEM(block, jnp.bfloat16),
            pltpu.VMEM((3, tokens, width), jnp.bfloat16),
            pltpu.VMEM((tokens, width), jnp.float32),
            pltpu.VMEM((2, tokens // 2, width), jnp.bfloat16),
            pltpu.VMEM((2, tokens, width), jnp.bfloat16),
            pltpu.VMEM((7, 1, tokens), jnp.float32),
            four, four, pair, pair, pair, pair, pair, pair, seven, seven,
        ],
        compiler_params=pltpu.CompilerParams(
            collective_id=0, has_side_effects=True, vmem_limit_bytes=40 << 20
        ),
    )(attended, out_weight, squares)


def shards(queries, key_rows, value_rows, log_decay, gate_logits, norm_gain, out_weight):
    rows_here = queries.shape[0]
    columns = queries.shape[1]
    head_count = columns // HEAD
    blocks = rows_here // BLOCK
    query_blocks = queries.reshape(blocks, BLOCK, head_count, HEAD)
    key_blocks = key_rows.reshape(blocks, BLOCK, head_count, HEAD)
    value_blocks = value_rows.reshape(blocks, BLOCK, head_count, HEAD)
    cumulative = jnp.cumsum(log_decay.reshape(head_count, blocks, BLOCK), axis=2)
    totals = cumulative[:, :, -1]
    causal = jnp.tril(jnp.ones((BLOCK, BLOCK), dtype=jnp.bool_))
    spread = cumulative[:, :, :, None] - cumulative[:, :, None, :]
    decays = jnp.where(causal, jnp.exp(jnp.where(causal, spread, 0.0)), 0.0)
    scores = jnp.einsum(
        "ntha,nsha->hnts", query_blocks, key_blocks, preferred_element_type=jnp.float32
    )
    weighted = (scores * decays).astype(jnp.bfloat16)
    inside = jnp.einsum(
        "hnts,nshb->nthb", weighted, value_blocks, preferred_element_type=jnp.float32
    )
    key_scale = jnp.exp(totals[:, :, None] - cumulative).transpose(1, 2, 0)[..., None]
    scaled_keys = (key_blocks.astype(jnp.float32) * key_scale).astype(jnp.bfloat16)
    block_states = jnp.einsum(
        "ntha,nthb->nhab", scaled_keys, value_blocks, preferred_element_type=jnp.float32
    )
    running = jnp.zeros((head_count, HEAD, HEAD), jnp.float32)
    decay_sum = jnp.zeros((head_count,), jnp.float32)
    local_before = []
    decay_before = []
    for block in range(blocks):
        local_before.append(running)
        decay_before.append(decay_sum)
        running = jnp.exp(totals[:, block])[:, None, None] * running + block_states[block]
        decay_sum = decay_sum + totals[:, block]
    incoming = exchange(running, decay_sum)
    starts = jnp.stack(
        [
            jnp.exp(decay_before[block])[:, None, None] * incoming + local_before[block]
            for block in range(blocks)
        ]
    )
    query_scale = jnp.exp(cumulative).transpose(1, 2, 0)[..., None]
    scaled_queries = query_blocks.astype(jnp.float32) * query_scale
    carried = jnp.einsum("ntha,nhab->nthb", scaled_queries, starts, precision=lax.Precision.HIGHEST)
    attention = (inside + carried).reshape(rows_here, columns)
    squares = jnp.sum(attention * attention, axis=1)
    gates = jax.nn.sigmoid(gate_logits.astype(jnp.float32))
    attended = (attention * norm_gain * gates).astype(jnp.bfloat16)
    return project(attended, out_weight, squares[None, :])


def solution(mesh):
    return jax.shard_map(
        shards,
        mesh=mesh,
        in_specs=(
            P("seq", "tp"),
            P("seq", "tp"),
            P("seq", "tp"),
            P("tp", "seq"),
            P("seq", "tp"),
            P("tp"),
            P("tp", None),
        ),
        out_specs=P("seq", "tp"),
        check_vma=False,
    )
```

```python
import jax
import jax.numpy as jnp
from jax import lax
from jax.experimental import pallas as pl
from jax.experimental.pallas import tpu as pltpu
from jax.sharding import PartitionSpec as P

HEAD = 128
HEADS = 32
BLOCK = 384


def exchange_kernel(
    state_ref, total_ref, first_total_ref, first_state_ref, cumulative_ref,
    q_ref, k_ref, v_ref, gate_ref, gain_ref, o_ref, sq_ref,
    attention, states, totals, row_state, row_total, rows_got, row_totals_got, back, mine,
    state_send, state_recv, total_send, total_recv, row_send, row_recv,
    row_total_send, row_total_recv, back_send, back_recv,
):
    me = lax.axis_index("seq")
    near = lax.rem(me, 8)
    far = lax.div(me, 8)
    head = lax.div(near, 2)

    def along(offset):
        return far * 8 + lax.rem(near + offset, 8)

    def across(offset):
        return lax.rem(far + offset, 8) * 8 + near

    barrier = pltpu.get_barrier_semaphore()
    for offset in range(1, 8):
        for peer in (along(offset), across(offset)):
            pl.semaphore_signal(
                barrier, inc=1, device_id={"seq": peer}, device_id_type=pl.DeviceIdType.MESH
            )
    pl.semaphore_wait(barrier, 14)

    def send(source, target, send_sem, recv_sem, to):
        copy = pltpu.make_async_remote_copy(
            src_ref=source, dst_ref=target, send_sem=send_sem, recv_sem=recv_sem,
            device_id={"seq": to}, device_id_type=pl.DeviceIdType.MESH,
        )
        copy.start()
        return copy

    order = (4, 3, 5, 2, 6, 1, 7)
    first = []
    for offset in order:
        i = offset - 1
        peer = lax.rem(near + offset, 8)
        first.append(
            send(total_ref, totals.at[near], total_send.at[i], total_recv.at[i], along(offset))
        )
        first.append(
            send(
                state_ref.at[peer], states.at[near],
                state_send.at[i], state_recv.at[i], along(offset),
            )
        )
    totals[near] = total_ref[...]
    states[near] = state_ref[near]
    by_token = jnp.transpose(cumulative_ref[...])
    causal = lax.broadcasted_iota(jnp.int32, (BLOCK, BLOCK), 0) >= lax.broadcasted_iota(
        jnp.int32, (BLOCK, BLOCK), 1
    )

    def inside(h):
        columns = slice(h * HEAD, (h + 1) * HEAD)
        for block in range(2):
            rows = slice(block * BLOCK, (block + 1) * BLOCK)
            scores = lax.dot_general(
                q_ref[rows, columns], k_ref[rows, columns], (((1,), (1,)), ((), ())),
                preferred_element_type=jnp.float32,
            )
            spread = by_token[rows, h : h + 1] - cumulative_ref[h : h + 1, rows]
            decay = jnp.where(causal, jnp.exp(jnp.where(causal, spread, 0.0)), 0.0)
            attention[rows, columns] = jnp.dot(
                (scores * decay).astype(jnp.bfloat16), v_ref[rows, columns],
                preferred_element_type=jnp.float32,
            )

    inside(0)
    inside(1)
    for copy in first:
        copy.wait_recv()
    decays = []
    pieces = []
    total = jnp.zeros(total_ref.shape, jnp.float32)
    running = jnp.zeros(row_state.shape, jnp.float32)
    for z in range(8):
        decay = jnp.exp(totals[z, pl.ds(head, 1), :])
        piece = states[z].astype(jnp.float32)
        running = decay * running + piece
        total = total + totals[z]
        decays.append(decay)
        pieces.append(piece)
    row_state[...] = running.astype(jnp.bfloat16)
    row_total[...] = total
    second = []
    for offset in order:
        i = offset - 1
        second.append(
            send(
                row_total, row_totals_got.at[far],
                row_total_send.at[i], row_total_recv.at[i], across(offset),
            )
        )
        second.append(
            send(row_state, rows_got.at[far], row_send.at[i], row_recv.at[i], across(offset))
        )
    rows_got[far] = row_state[...]
    row_totals_got[far] = row_total[...]
    inside(2)
    for copy in second:
        copy.wait_recv()
    running = jnp.zeros(row_state.shape, jnp.float32)
    for y in range(8):
        decay = jnp.exp(row_totals_got[y, pl.ds(head, 1), :])
        moved = decay * running + rows_got[y].astype(jnp.float32)
        running = jnp.where(y < far, moved, running)
    for z in range(8):
        back[z] = running.astype(jnp.bfloat16)
        running = decays[z] * running + pieces[z]
    third = []
    for offset in order:
        i = offset - 1
        peer = lax.rem(near + offset, 8)
        third.append(
            send(back.at[peer], mine.at[near], back_send.at[i], back_recv.at[i], along(offset))
        )
    mine[near] = back[near]
    inside(3)
    for copy in third:
        copy.wait_recv()
    squares = [jnp.zeros((BLOCK, 1), jnp.float32) for block in range(2)]
    for h in range(HEADS // 8):
        columns = slice(h * HEAD, (h + 1) * HEAD)
        start = mine[2 * h : 2 * h + 2].astype(jnp.float32).reshape(HEAD, HEAD)
        for block in range(2):
            rows = slice(block * BLOCK, (block + 1) * BLOCK)
            if block == 1:
                start = jnp.exp(first_total_ref[h : h + 1, :]) * start + first_state_ref[h]
            query = q_ref[rows, columns].astype(jnp.float32) * jnp.exp(by_token[rows, h : h + 1])
            full = attention[rows, columns] + jnp.dot(
                query, start, precision=lax.Precision.HIGHEST,
                preferred_element_type=jnp.float32,
            )
            squares[block] = squares[block] + jnp.sum(full * full, axis=1, keepdims=True)
            gates = jax.nn.sigmoid(gate_ref[rows, columns].astype(jnp.float32))
            o_ref[rows, columns] = (full * gain_ref[:, columns] * gates).astype(jnp.bfloat16)
    for block in range(2):
        spread = jnp.broadcast_to(squares[block], (BLOCK, HEAD))
        sq_ref[:, block * BLOCK : (block + 1) * BLOCK] = jnp.transpose(spread)[:1]
    for copy in first + second + third:
        copy.wait_send()


def exchange(
    running, decay_sum, first_total, first_state, cumulative,
    queries, key_rows, value_rows, gate_logits, norm_gain,
):
    head_count = running.shape[0]
    rows = head_count * HEAD // 8
    pieces = running.astype(jnp.bfloat16).reshape(8, rows, HEAD)

    def spread_out(total):
        return jnp.pad(
            jnp.broadcast_to(total[:, None], (head_count, HEAD)), ((0, 8 - head_count), (0, 0))
        )

    tokens, columns = queries.shape
    cumulative = jnp.pad(cumulative.reshape(head_count, tokens), ((0, 8 - head_count), (0, 0)))
    seven = pltpu.SemaphoreType.DMA((7,))
    vmem = pl.BlockSpec(memory_space=pltpu.VMEM)
    block = pltpu.VMEM((8, rows, HEAD), jnp.bfloat16)
    sums = pltpu.VMEM((8, 8, HEAD), jnp.float32)
    return pl.pallas_call(
        exchange_kernel,
        out_shape=[
            jax.ShapeDtypeStruct((tokens, columns), jnp.bfloat16),
            jax.ShapeDtypeStruct((1, tokens), jnp.float32),
        ],
        in_specs=[vmem] * 10,
        out_specs=[vmem] * 2,
        scratch_shapes=[
            pltpu.VMEM((tokens, columns), jnp.float32),
            block, sums,
            pltpu.VMEM((rows, HEAD), jnp.bfloat16),
            pltpu.VMEM((8, HEAD), jnp.float32),
            block, sums, block, block,
        ] + [seven] * 10,
        compiler_params=pltpu.CompilerParams(collective_id=1, has_side_effects=True),
    )(
        pieces, spread_out(decay_sum), spread_out(first_total), first_state, cumulative,
        queries, key_rows, value_rows, gate_logits, norm_gain[None, :],
    )


def project_kernel(
    a_ref, w_ref, sq_ref, o_ref,
    give, got, held, own, relay, landed, squares,
    give_send, give_recv, far_send, far_recv, near_send, near_recv,
    last_send, last_recv, sq_send, sq_recv,
):
    tokens, width = o_ref.shape
    half = tokens // 2
    tile = tokens // 3
    me = lax.axis_index("tp")
    core = lax.rem(me, 2)
    chip = lax.div(me, 2)

    def device(step, which):
        return lax.rem(chip + step, 4) * 2 + which

    sibling = device(0, 1 - core)
    right, left = device(1, core), device(3, core)

    barrier = pltpu.get_barrier_semaphore()
    for offset in range(1, 8):
        pl.semaphore_signal(
            barrier, inc=1, device_id={"tp": lax.rem(me + offset, 8)},
            device_id_type=pl.DeviceIdType.MESH,
        )
    pl.semaphore_wait(barrier, 7)

    def send(source, target, send_sem, recv_sem, to):
        copy = pltpu.make_async_remote_copy(
            src_ref=source, dst_ref=target, send_sem=send_sem, recv_sem=recv_sem,
            device_id={"tp": to}, device_id_type=pl.DeviceIdType.MESH,
        )
        copy.start()
        return copy

    copies = []
    sq_copies = [
        send(sq_ref, squares.at[i], sq_send.at[i], sq_recv.at[i], lax.rem(me + i + 1, 8))
        for i in range(7)
    ]

    def tiles(body):
        def step(i, carry):
            body(pl.ds(pl.multiple_of(i * tile, tile), tile))
            return carry

        lax.fori_loop(0, 3, step, 0)

    def product(dest, rows):
        columns = pl.ds(pl.multiple_of(dest * width, 128), width)
        return jnp.dot(a_ref[rows, :], w_ref[:, columns], preferred_element_type=jnp.float32)

    steps = (2, 1, 3, 0)
    gives = []

    def hand_over(k):
        def body(rows):
            give[k, rows, :] = product(device(steps[k], 1 - core), rows).astype(jnp.bfloat16)

        tiles(body)
        gives.append(send(give.at[k], got.at[k], give_send.at[k], give_recv.at[k], sibling))

    def gather(k, target, dtype):
        def first(rows):
            own[rows, :] = product(device(steps[k], core), rows)

        tiles(first)
        gives[k].wait_recv()

        def second(rows):
            total = own[rows, :] + got[k, rows, :].astype(jnp.float32)
            if dtype is None:
                own[rows, :] = total
            else:
                target[k, rows, :] = total.astype(dtype)

        tiles(second)

    top, bottom = pl.ds(0, half), pl.ds(half, half)
    hand_over(0)
    hand_over(1)
    gather(0, held, jnp.bfloat16)
    far_right = send(held.at[0, top], relay.at[0], far_send.at[0], far_recv.at[0], right)
    far_left = send(held.at[0, bottom], relay.at[1], far_send.at[1], far_recv.at[1], left)
    hand_over(2)
    gather(1, held, jnp.bfloat16)
    near_right = send(
        held.at[1, bottom], landed.at[0, bottom], near_send.at[0], near_recv.at[0], right
    )
    hand_over(3)
    gather(2, held, jnp.bfloat16)
    near_left = send(held.at[2, top], landed.at[1, top], near_send.at[1], near_recv.at[1], left)
    gather(3, None, None)

    def merge(k, start, slot):
        piece = half // 3

        def step(i, carry):
            rows = pl.ds(pl.multiple_of(start + i * piece, piece), piece)
            here = pl.ds(pl.multiple_of(i * piece, piece), piece)
            total = held[k, rows, :].astype(jnp.float32) + relay[slot, here, :].astype(jnp.float32)
            held[k, rows, :] = total.astype(jnp.bfloat16)
            return carry

        lax.fori_loop(0, 3, step, 0)

    far_right.wait_recv()
    merge(1, 0, 0)
    last_right = send(held.at[1, top], landed.at[0, top], last_send.at[0], last_recv.at[0], right)
    far_left.wait_recv()
    merge(2, half, 1)
    last_left = send(
        held.at[2, bottom], landed.at[1, bottom], last_send.at[1], last_recv.at[1], left
    )
    total = sq_ref[...]
    for i in range(7):
        sq_copies[i].wait_recv()
        total = total + squares[i]
    scale = lax.rsqrt(total / (HEADS * HEAD) + 1e-06)
    scale = jnp.transpose(jnp.broadcast_to(scale, (8, tokens)))[:, :1]
    near_right.wait_recv()
    near_left.wait_recv()
    last_right.wait_recv()
    last_left.wait_recv()
    for i in range(3):
        rows = slice(i * tile, (i + 1) * tile)
        summed = (
            own[rows, :]
            + landed[0, rows, :].astype(jnp.float32)
            + landed[1, rows, :].astype(jnp.float32)
        )
        o_ref[rows, :] = (summed * scale[rows]).astype(o_ref.dtype)
    for copy in sq_copies + gives + [
        far_right, far_left, near_right, near_left, last_right, last_left
    ]:
        copy.wait_send()


def project(attended, out_weight, squares):
    tokens = attended.shape[0]
    width = out_weight.shape[1] // 8
    block = (4, tokens, width)
    pair = pltpu.SemaphoreType.DMA((2,))
    four = pltpu.SemaphoreType.DMA((4,))
    seven = pltpu.SemaphoreType.DMA((7,))
    vmem = pl.BlockSpec(memory_space=pltpu.VMEM)
    return pl.pallas_call(
        project_kernel,
        out_shape=jax.ShapeDtypeStruct((tokens, width), jnp.bfloat16),
        in_specs=[vmem] * 3,
        out_specs=vmem,
        scratch_shapes=[
            pltpu.VMEM(block, jnp.bfloat16),
            pltpu.VMEM(block, jnp.bfloat16),
            pltpu.VMEM((3, tokens, width), jnp.bfloat16),
            pltpu.VMEM((tokens, width), jnp.float32),
            pltpu.VMEM((2, tokens // 2, width), jnp.bfloat16),
            pltpu.VMEM((2, tokens, width), jnp.bfloat16),
            pltpu.VMEM((7, 1, tokens), jnp.float32),
            four, four, pair, pair, pair, pair, pair, pair, seven, seven,
        ],
        compiler_params=pltpu.CompilerParams(
            collective_id=0, has_side_effects=True, vmem_limit_bytes=40 << 20
        ),
    )(attended, out_weight, squares)


def shards(queries, key_rows, value_rows, log_decay, gate_logits, norm_gain, out_weight):
    rows_here = queries.shape[0]
    columns = queries.shape[1]
    head_count = columns // HEAD
    blocks = rows_here // BLOCK
    key_blocks = key_rows.reshape(blocks, BLOCK, head_count, HEAD)
    value_blocks = value_rows.reshape(blocks, BLOCK, head_count, HEAD)
    cumulative = jnp.cumsum(log_decay.reshape(head_count, blocks, BLOCK), axis=2)
    totals = cumulative[:, :, -1]
    key_scale = jnp.exp(totals[:, :, None] - cumulative).transpose(1, 2, 0)[..., None]
    scaled_keys = (key_blocks.astype(jnp.float32) * key_scale).astype(jnp.bfloat16)
    block_states = jnp.einsum(
        "ntha,nthb->nhab", scaled_keys, value_blocks, preferred_element_type=jnp.float32
    )
    running = jnp.zeros((head_count, HEAD, HEAD), jnp.float32)
    decay_sum = jnp.zeros((head_count,), jnp.float32)
    for block in range(blocks):
        running = jnp.exp(totals[:, block])[:, None, None] * running + block_states[block]
        decay_sum = decay_sum + totals[:, block]
    attended, squares = exchange(
        running, decay_sum, totals[:, 0], block_states[0], cumulative,
        queries, key_rows, value_rows, gate_logits, norm_gain,
    )
    return project(attended, out_weight, squares)


def solution(mesh):
    return jax.shard_map(
        shards,
        mesh=mesh,
        in_specs=(
            P("seq", "tp"),
            P("seq", "tp"),
            P("seq", "tp"),
            P("tp", "seq"),
            P("seq", "tp"),
            P("tp"),
            P("tp", None),
        ),
        out_specs=P("seq", "tp"),
        check_vma=False,
    )
```

```python
import jax
import jax.numpy as jnp
from jax import lax
from jax.experimental import pallas as pl
from jax.experimental.pallas import tpu as pltpu
from jax.sharding import PartitionSpec as P

HEAD = 128
HEADS = 32
BLOCK = 384


def exchange_kernel(
    decay_ref, q_ref, k_ref, v_ref, gate_ref, gain_ref, o_ref, sq_ref,
    state_ref, total_ref, first_total_ref, first_state_ref, cumulative_ref, attention, states, totals, row_state, row_total, rows_got, row_totals_got, back, mine,
    state_send, state_recv, total_send, total_recv, row_send, row_recv,
    row_total_send, row_total_recv, back_send, back_recv,
):
    me = lax.axis_index("seq")
    near = lax.rem(me, 8)
    far = lax.div(me, 8)
    head = lax.div(near, 2)

    def along(offset):
        return far * 8 + lax.rem(near + offset, 8)

    def across(offset):
        return lax.rem(far + offset, 8) * 8 + near

    barrier = pltpu.get_barrier_semaphore()
    for offset in range(1, 8):
        for peer in (along(offset), across(offset)):
            pl.semaphore_signal(
                barrier, inc=1, device_id={"seq": peer}, device_id_type=pl.DeviceIdType.MESH
            )
    row_index = lax.broadcasted_iota(jnp.int32, (BLOCK, BLOCK), 0)
    column_index = lax.broadcasted_iota(jnp.int32, (BLOCK, BLOCK), 1)
    causal = row_index >= column_index
    upto = jnp.where(row_index <= column_index, 1.0, 0.0).astype(jnp.float32)
    heads = HEADS // 8
    cumulative_ref[...] = jnp.zeros(cumulative_ref.shape, jnp.float32)
    for block in range(2):
        rows = slice(block * BLOCK, (block + 1) * BLOCK)
        cumulative_ref[:heads, rows] = jnp.dot(
            decay_ref[:, rows], upto, precision=lax.Precision.HIGHEST,
            preferred_element_type=jnp.float32,
        )
    by_token = jnp.transpose(cumulative_ref[...])
    ends = [
        jnp.broadcast_to(
            cumulative_ref[:, (block + 1) * BLOCK - 1 : (block + 1) * BLOCK], total_ref.shape
        )
        for block in range(2)
    ]
    first_total_ref[...] = ends[0]
    total_ref[...] = ends[0] + ends[1]
    for h in range(heads):
        columns = slice(h * HEAD, (h + 1) * HEAD)
        sums = []
        for block in range(2):
            rows = slice(block * BLOCK, (block + 1) * BLOCK)
            scale = jnp.exp(ends[block][h : h + 1, :] - by_token[rows, h : h + 1])
            scaled = (k_ref[rows, columns].astype(jnp.float32) * scale).astype(jnp.bfloat16)
            sums.append(
                lax.dot_general(
                    scaled, v_ref[rows, columns], (((0,), (0,)), ((), ())),
                    preferred_element_type=jnp.float32,
                )
            )
        first_state_ref[h] = sums[0]
        whole = (jnp.exp(ends[1][h : h + 1, :]) * sums[0] + sums[1]).astype(jnp.bfloat16)
        state_ref[2 * h] = whole[: HEAD // 2]
        state_ref[2 * h + 1] = whole[HEAD // 2 :]
    pl.semaphore_wait(barrier, 14)

    def send(source, target, send_sem, recv_sem, to):
        copy = pltpu.make_async_remote_copy(
            src_ref=source, dst_ref=target, send_sem=send_sem, recv_sem=recv_sem,
            device_id={"seq": to}, device_id_type=pl.DeviceIdType.MESH,
        )
        copy.start()
        return copy

    order = (4, 3, 5, 2, 6, 1, 7)
    first = []
    for offset in order:
        i = offset - 1
        peer = lax.rem(near + offset, 8)
        first.append(
            send(total_ref, totals.at[near], total_send.at[i], total_recv.at[i], along(offset))
        )
        first.append(
            send(
                state_ref.at[peer], states.at[near],
                state_send.at[i], state_recv.at[i], along(offset),
            )
        )
    totals[near] = total_ref[...]
    states[near] = state_ref[near]

    def inside(h):
        columns = slice(h * HEAD, (h + 1) * HEAD)
        for block in range(2):
            rows = slice(block * BLOCK, (block + 1) * BLOCK)
            scores = lax.dot_general(
                q_ref[rows, columns], k_ref[rows, columns], (((1,), (1,)), ((), ())),
                preferred_element_type=jnp.float32,
            )
            spread = by_token[rows, h : h + 1] - cumulative_ref[h : h + 1, rows]
            decay = jnp.where(causal, jnp.exp(jnp.where(causal, spread, 0.0)), 0.0)
            attention[rows, columns] = jnp.dot(
                (scores * decay).astype(jnp.bfloat16), v_ref[rows, columns],
                preferred_element_type=jnp.float32,
            )

    inside(0)
    inside(1)
    for copy in first:
        copy.wait_recv()
    decays = []
    pieces = []
    total = jnp.zeros(total_ref.shape, jnp.float32)
    running = jnp.zeros(row_state.shape, jnp.float32)
    for z in range(8):
        decay = jnp.exp(totals[z, pl.ds(head, 1), :])
        piece = states[z].astype(jnp.float32)
        running = decay * running + piece
        total = total + totals[z]
        decays.append(decay)
        pieces.append(piece)
    row_state[...] = running.astype(jnp.bfloat16)
    row_total[...] = total
    second = []
    for offset in order:
        i = offset - 1
        second.append(
            send(
                row_total, row_totals_got.at[far],
                row_total_send.at[i], row_total_recv.at[i], across(offset),
            )
        )
        second.append(
            send(row_state, rows_got.at[far], row_send.at[i], row_recv.at[i], across(offset))
        )
    rows_got[far] = row_state[...]
    row_totals_got[far] = row_total[...]
    inside(2)
    for copy in second:
        copy.wait_recv()
    running = jnp.zeros(row_state.shape, jnp.float32)
    for y in range(8):
        decay = jnp.exp(row_totals_got[y, pl.ds(head, 1), :])
        moved = decay * running + rows_got[y].astype(jnp.float32)
        running = jnp.where(y < far, moved, running)
    for z in range(8):
        back[z] = running.astype(jnp.bfloat16)
        running = decays[z] * running + pieces[z]
    third = []
    for offset in order:
        i = offset - 1
        peer = lax.rem(near + offset, 8)
        third.append(
            send(back.at[peer], mine.at[near], back_send.at[i], back_recv.at[i], along(offset))
        )
    mine[near] = back[near]
    inside(3)
    for copy in third:
        copy.wait_recv()
    squares = [jnp.zeros((BLOCK, 1), jnp.float32) for block in range(2)]
    for h in range(HEADS // 8):
        columns = slice(h * HEAD, (h + 1) * HEAD)
        start = mine[2 * h : 2 * h + 2].astype(jnp.float32).reshape(HEAD, HEAD)
        for block in range(2):
            rows = slice(block * BLOCK, (block + 1) * BLOCK)
            if block == 1:
                start = jnp.exp(first_total_ref[h : h + 1, :]) * start + first_state_ref[h]
            query = q_ref[rows, columns].astype(jnp.float32) * jnp.exp(by_token[rows, h : h + 1])
            full = attention[rows, columns] + jnp.dot(
                query, start, precision=lax.Precision.HIGHEST,
                preferred_element_type=jnp.float32,
            )
            squares[block] = squares[block] + jnp.sum(full * full, axis=1, keepdims=True)
            gates = jax.nn.sigmoid(gate_ref[rows, columns].astype(jnp.float32))
            o_ref[rows, columns] = (full * gain_ref[:, columns] * gates).astype(jnp.bfloat16)
    for block in range(2):
        spread = jnp.broadcast_to(squares[block], (BLOCK, HEAD))
        sq_ref[:, block * BLOCK : (block + 1) * BLOCK] = jnp.transpose(spread)[:1]
    for copy in first + second + third:
        copy.wait_send()


def exchange(log_decay, queries, key_rows, value_rows, gate_logits, norm_gain):
    tokens, columns = queries.shape
    rows = columns // 8
    seven = pltpu.SemaphoreType.DMA((7,))
    vmem = pl.BlockSpec(memory_space=pltpu.VMEM)
    block = pltpu.VMEM((8, rows, HEAD), jnp.bfloat16)
    sums = pltpu.VMEM((8, 8, HEAD), jnp.float32)
    return pl.pallas_call(
        exchange_kernel,
        out_shape=[
            jax.ShapeDtypeStruct((tokens, columns), jnp.bfloat16),
            jax.ShapeDtypeStruct((1, tokens), jnp.float32),
        ],
        in_specs=[vmem] * 6,
        out_specs=[vmem] * 2,
        scratch_shapes=[
            block,
            pltpu.VMEM((8, HEAD), jnp.float32),
            pltpu.VMEM((8, HEAD), jnp.float32),
            pltpu.VMEM((columns // HEAD, HEAD, HEAD), jnp.float32),
            pltpu.VMEM((8, tokens), jnp.float32),
            pltpu.VMEM((tokens, columns), jnp.float32),
            block, sums,
            pltpu.VMEM((rows, HEAD), jnp.bfloat16),
            pltpu.VMEM((8, HEAD), jnp.float32),
            block, sums, block, block,
        ] + [seven] * 10,
        compiler_params=pltpu.CompilerParams(collective_id=1, has_side_effects=True),
    )(log_decay, queries, key_rows, value_rows, gate_logits, norm_gain[None, :])


def project_kernel(
    a_ref, w_ref, sq_ref, o_ref,
    give, got, held, own, relay, landed, squares,
    give_send, give_recv, far_send, far_recv, near_send, near_recv,
    last_send, last_recv, sq_send, sq_recv,
):
    tokens, width = o_ref.shape
    half = tokens // 2
    tile = tokens // 3
    me = lax.axis_index("tp")
    core = lax.rem(me, 2)
    chip = lax.div(me, 2)

    def device(step, which):
        return lax.rem(chip + step, 4) * 2 + which

    sibling = device(0, 1 - core)
    right, left = device(1, core), device(3, core)

    barrier = pltpu.get_barrier_semaphore()
    for offset in range(1, 8):
        pl.semaphore_signal(
            barrier, inc=1, device_id={"tp": lax.rem(me + offset, 8)},
            device_id_type=pl.DeviceIdType.MESH,
        )
    pl.semaphore_wait(barrier, 7)

    def send(source, target, send_sem, recv_sem, to):
        copy = pltpu.make_async_remote_copy(
            src_ref=source, dst_ref=target, send_sem=send_sem, recv_sem=recv_sem,
            device_id={"tp": to}, device_id_type=pl.DeviceIdType.MESH,
        )
        copy.start()
        return copy

    copies = []
    sq_copies = [
        send(sq_ref, squares.at[i], sq_send.at[i], sq_recv.at[i], lax.rem(me + i + 1, 8))
        for i in range(7)
    ]

    def tiles(body):
        def step(i, carry):
            body(pl.ds(pl.multiple_of(i * tile, tile), tile))
            return carry

        lax.fori_loop(0, 3, step, 0)

    def product(dest, rows):
        columns = pl.ds(pl.multiple_of(dest * width, 128), width)
        return jnp.dot(a_ref[rows, :], w_ref[:, columns], preferred_element_type=jnp.float32)

    steps = (2, 1, 3, 0)
    gives = []

    def hand_over(k):
        def body(rows):
            give[k, rows, :] = product(device(steps[k], 1 - core), rows).astype(jnp.bfloat16)

        tiles(body)
        gives.append(send(give.at[k], got.at[k], give_send.at[k], give_recv.at[k], sibling))

    def gather(k, target, dtype):
        def first(rows):
            own[rows, :] = product(device(steps[k], core), rows)

        tiles(first)
        gives[k].wait_recv()

        def second(rows):
            total = own[rows, :] + got[k, rows, :].astype(jnp.float32)
            if dtype is None:
                own[rows, :] = total
            else:
                target[k, rows, :] = total.astype(dtype)

        tiles(second)

    top, bottom = pl.ds(0, half), pl.ds(half, half)
    hand_over(0)
    hand_over(1)
    gather(0, held, jnp.bfloat16)
    far_right = send(held.at[0, top], relay.at[0], far_send.at[0], far_recv.at[0], right)
    far_left = send(held.at[0, bottom], relay.at[1], far_send.at[1], far_recv.at[1], left)
    hand_over(2)
    gather(1, held, jnp.bfloat16)
    near_right = send(
        held.at[1, bottom], landed.at[0, bottom], near_send.at[0], near_recv.at[0], right
    )
    hand_over(3)
    gather(2, held, jnp.bfloat16)
    near_left = send(held.at[2, top], landed.at[1, top], near_send.at[1], near_recv.at[1], left)
    gather(3, None, None)

    def merge(k, start, slot):
        piece = half // 3

        def step(i, carry):
            rows = pl.ds(pl.multiple_of(start + i * piece, piece), piece)
            here = pl.ds(pl.multiple_of(i * piece, piece), piece)
            total = held[k, rows, :].astype(jnp.float32) + relay[slot, here, :].astype(jnp.float32)
            held[k, rows, :] = total.astype(jnp.bfloat16)
            return carry

        lax.fori_loop(0, 3, step, 0)

    far_right.wait_recv()
    merge(1, 0, 0)
    last_right = send(held.at[1, top], landed.at[0, top], last_send.at[0], last_recv.at[0], right)
    far_left.wait_recv()
    merge(2, half, 1)
    last_left = send(
        held.at[2, bottom], landed.at[1, bottom], last_send.at[1], last_recv.at[1], left
    )
    total = sq_ref[...]
    for i in range(7):
        sq_copies[i].wait_recv()
        total = total + squares[i]
    scale = lax.rsqrt(total / (HEADS * HEAD) + 1e-06)
    scale = jnp.transpose(jnp.broadcast_to(scale, (8, tokens)))[:, :1]
    near_right.wait_recv()
    near_left.wait_recv()
    last_right.wait_recv()
    last_left.wait_recv()
    for i in range(3):
        rows = slice(i * tile, (i + 1) * tile)
        summed = (
            own[rows, :]
            + landed[0, rows, :].astype(jnp.float32)
            + landed[1, rows, :].astype(jnp.float32)
        )
        o_ref[rows, :] = (summed * scale[rows]).astype(o_ref.dtype)
    for copy in sq_copies + gives + [
        far_right, far_left, near_right, near_left, last_right, last_left
    ]:
        copy.wait_send()


def project(attended, out_weight, squares):
    tokens = attended.shape[0]
    width = out_weight.shape[1] // 8
    block = (4, tokens, width)
    pair = pltpu.SemaphoreType.DMA((2,))
    four = pltpu.SemaphoreType.DMA((4,))
    seven = pltpu.SemaphoreType.DMA((7,))
    vmem = pl.BlockSpec(memory_space=pltpu.VMEM)
    return pl.pallas_call(
        project_kernel,
        out_shape=jax.ShapeDtypeStruct((tokens, width), jnp.bfloat16),
        in_specs=[vmem] * 3,
        out_specs=vmem,
        scratch_shapes=[
            pltpu.VMEM(block, jnp.bfloat16),
            pltpu.VMEM(block, jnp.bfloat16),
            pltpu.VMEM((3, tokens, width), jnp.bfloat16),
            pltpu.VMEM((tokens, width), jnp.float32),
            pltpu.VMEM((2, tokens // 2, width), jnp.bfloat16),
            pltpu.VMEM((2, tokens, width), jnp.bfloat16),
            pltpu.VMEM((7, 1, tokens), jnp.float32),
            four, four, pair, pair, pair, pair, pair, pair, seven, seven,
        ],
        compiler_params=pltpu.CompilerParams(
            collective_id=0, has_side_effects=True, vmem_limit_bytes=40 << 20
        ),
    )(attended, out_weight, squares)


def shards(queries, key_rows, value_rows, log_decay, gate_logits, norm_gain, out_weight):
    attended, squares = exchange(
        log_decay, queries, key_rows, value_rows, gate_logits, norm_gain
    )
    return project(attended, out_weight, squares)


def solution(mesh):
    return jax.shard_map(
        shards,
        mesh=mesh,
        in_specs=(
            P("seq", "tp"),
            P("seq", "tp"),
            P("seq", "tp"),
            P("tp", "seq"),
            P("seq", "tp"),
            P("tp"),
            P("tp", None),
        ),
        out_specs=P("seq", "tp"),
        check_vma=False,
    )
```

```python
import jax
import jax.numpy as jnp
from jax import lax
from jax.experimental import pallas as pl
from jax.experimental.pallas import tpu as pltpu
from jax.sharding import PartitionSpec as P

HEAD = 128
HEADS = 32
BLOCK = 384


def exchange_kernel(
    decay_ref, q_ref, k_ref, v_ref, gate_ref, gain_ref, o_ref, sq_ref,
    state_ref, total_ref, first_total_ref, first_state_ref, cumulative_ref, attention, factor, scaled_q, states, totals, row_state, row_total, rows_got, row_totals_got, back, mine,
    state_send, state_recv, total_send, total_recv, row_send, row_recv,
    row_total_send, row_total_recv, back_send, back_recv,
):
    me = lax.axis_index("seq")
    near = lax.rem(me, 8)
    far = lax.div(me, 8)
    head = lax.div(near, 2)

    def along(offset):
        return far * 8 + lax.rem(near + offset, 8)

    def across(offset):
        return lax.rem(far + offset, 8) * 8 + near

    barrier = pltpu.get_barrier_semaphore()
    for offset in range(1, 8):
        for peer in (along(offset), across(offset)):
            pl.semaphore_signal(
                barrier, inc=1, device_id={"seq": peer}, device_id_type=pl.DeviceIdType.MESH
            )
    row_index = lax.broadcasted_iota(jnp.int32, (BLOCK, BLOCK), 0)
    column_index = lax.broadcasted_iota(jnp.int32, (BLOCK, BLOCK), 1)
    causal = row_index >= column_index
    upto = jnp.where(row_index <= column_index, 1.0, 0.0).astype(jnp.float32)
    heads = HEADS // 8
    cumulative_ref[...] = jnp.zeros(cumulative_ref.shape, jnp.float32)
    for block in range(2):
        rows = slice(block * BLOCK, (block + 1) * BLOCK)
        cumulative_ref[:heads, rows] = jnp.dot(
            decay_ref[:, rows], upto, precision=lax.Precision.HIGHEST,
            preferred_element_type=jnp.float32,
        )
    by_token = jnp.transpose(cumulative_ref[...])
    ends = [
        jnp.broadcast_to(
            cumulative_ref[:, (block + 1) * BLOCK - 1 : (block + 1) * BLOCK], total_ref.shape
        )
        for block in range(2)
    ]
    first_total_ref[...] = ends[0]
    total_ref[...] = ends[0] + ends[1]
    for h in range(heads):
        columns = slice(h * HEAD, (h + 1) * HEAD)
        sums = []
        for block in range(2):
            rows = slice(block * BLOCK, (block + 1) * BLOCK)
            scale = jnp.exp(ends[block][h : h + 1, :] - by_token[rows, h : h + 1])
            scaled = (k_ref[rows, columns].astype(jnp.float32) * scale).astype(jnp.bfloat16)
            sums.append(
                lax.dot_general(
                    scaled, v_ref[rows, columns], (((0,), (0,)), ((), ())),
                    preferred_element_type=jnp.float32,
                )
            )
        first_state_ref[h] = sums[0]
        whole = (jnp.exp(ends[1][h : h + 1, :]) * sums[0] + sums[1]).astype(jnp.bfloat16)
        state_ref[2 * h] = whole[: HEAD // 2]
        state_ref[2 * h + 1] = whole[HEAD // 2 :]
    pl.semaphore_wait(barrier, 14)

    def send(source, target, send_sem, recv_sem, to):
        copy = pltpu.make_async_remote_copy(
            src_ref=source, dst_ref=target, send_sem=send_sem, recv_sem=recv_sem,
            device_id={"seq": to}, device_id_type=pl.DeviceIdType.MESH,
        )
        copy.start()
        return copy

    order = (4, 3, 5, 2, 6, 1, 7)
    first = []
    for offset in order:
        i = offset - 1
        peer = lax.rem(near + offset, 8)
        first.append(
            send(total_ref, totals.at[near], total_send.at[i], total_recv.at[i], along(offset))
        )
        first.append(
            send(
                state_ref.at[peer], states.at[near],
                state_send.at[i], state_recv.at[i], along(offset),
            )
        )
    totals[near] = total_ref[...]
    states[near] = state_ref[near]

    def inside(h):
        columns = slice(h * HEAD, (h + 1) * HEAD)
        for block in range(2):
            rows = slice(block * BLOCK, (block + 1) * BLOCK)
            scores = lax.dot_general(
                q_ref[rows, columns], k_ref[rows, columns], (((1,), (1,)), ((), ())),
                preferred_element_type=jnp.float32,
            )
            gates = jax.nn.sigmoid(gate_ref[rows, columns].astype(jnp.float32))
            factor[rows, columns] = gain_ref[:, columns] * gates
            scaled_q[rows, columns] = q_ref[rows, columns].astype(jnp.float32) * jnp.exp(
                by_token[rows, h : h + 1]
            )
            spread = by_token[rows, h : h + 1] - cumulative_ref[h : h + 1, rows]
            decay = jnp.where(causal, jnp.exp(jnp.where(causal, spread, 0.0)), 0.0)
            attention[rows, columns] = jnp.dot(
                (scores * decay).astype(jnp.bfloat16), v_ref[rows, columns],
                preferred_element_type=jnp.float32,
            )

    inside(0)
    inside(1)
    for copy in first:
        copy.wait_recv()
    decays = []
    pieces = []
    total = jnp.zeros(total_ref.shape, jnp.float32)
    running = jnp.zeros(row_state.shape, jnp.float32)
    for z in range(8):
        decay = jnp.exp(totals[z, pl.ds(head, 1), :])
        piece = states[z].astype(jnp.float32)
        running = decay * running + piece
        total = total + totals[z]
        decays.append(decay)
        pieces.append(piece)
    row_state[...] = running.astype(jnp.bfloat16)
    row_total[...] = total
    second = []
    for offset in order:
        i = offset - 1
        second.append(
            send(
                row_total, row_totals_got.at[far],
                row_total_send.at[i], row_total_recv.at[i], across(offset),
            )
        )
        second.append(
            send(row_state, rows_got.at[far], row_send.at[i], row_recv.at[i], across(offset))
        )
    rows_got[far] = row_state[...]
    row_totals_got[far] = row_total[...]
    inside(2)
    for copy in second:
        copy.wait_recv()
    running = jnp.zeros(row_state.shape, jnp.float32)
    for y in range(8):
        decay = jnp.exp(row_totals_got[y, pl.ds(head, 1), :])
        moved = decay * running + rows_got[y].astype(jnp.float32)
        running = jnp.where(y < far, moved, running)
    for z in range(8):
        back[z] = running.astype(jnp.bfloat16)
        running = decays[z] * running + pieces[z]
    third = []
    for offset in order:
        i = offset - 1
        peer = lax.rem(near + offset, 8)
        third.append(
            send(back.at[peer], mine.at[near], back_send.at[i], back_recv.at[i], along(offset))
        )
    mine[near] = back[near]
    inside(3)
    for copy in third:
        copy.wait_recv()
    squares = [jnp.zeros((BLOCK, 1), jnp.float32) for block in range(2)]
    for h in range(HEADS // 8):
        columns = slice(h * HEAD, (h + 1) * HEAD)
        start = mine[2 * h : 2 * h + 2].astype(jnp.float32).reshape(HEAD, HEAD)
        for block in range(2):
            rows = slice(block * BLOCK, (block + 1) * BLOCK)
            if block == 1:
                start = jnp.exp(first_total_ref[h : h + 1, :]) * start + first_state_ref[h]
            full = attention[rows, columns] + jnp.dot(
                scaled_q[rows, columns], start, precision=lax.Precision.HIGHEST,
                preferred_element_type=jnp.float32,
            )
            squares[block] = squares[block] + jnp.sum(full * full, axis=1, keepdims=True)
            o_ref[rows, columns] = (full * factor[rows, columns]).astype(jnp.bfloat16)
    for block in range(2):
        spread = jnp.broadcast_to(squares[block], (BLOCK, HEAD))
        sq_ref[:, block * BLOCK : (block + 1) * BLOCK] = jnp.transpose(spread)[:1]
    for copy in first + second + third:
        copy.wait_send()


def exchange(log_decay, queries, key_rows, value_rows, gate_logits, norm_gain):
    tokens, columns = queries.shape
    rows = columns // 8
    seven = pltpu.SemaphoreType.DMA((7,))
    vmem = pl.BlockSpec(memory_space=pltpu.VMEM)
    block = pltpu.VMEM((8, rows, HEAD), jnp.bfloat16)
    sums = pltpu.VMEM((8, 8, HEAD), jnp.float32)
    return pl.pallas_call(
        exchange_kernel,
        out_shape=[
            jax.ShapeDtypeStruct((tokens, columns), jnp.bfloat16),
            jax.ShapeDtypeStruct((1, tokens), jnp.float32),
        ],
        in_specs=[vmem] * 6,
        out_specs=[vmem] * 2,
        scratch_shapes=[
            block,
            pltpu.VMEM((8, HEAD), jnp.float32),
            pltpu.VMEM((8, HEAD), jnp.float32),
            pltpu.VMEM((columns // HEAD, HEAD, HEAD), jnp.float32),
            pltpu.VMEM((8, tokens), jnp.float32),
            pltpu.VMEM((tokens, columns), jnp.float32),
            pltpu.VMEM((tokens, columns), jnp.float32),
            pltpu.VMEM((tokens, columns), jnp.float32),
            block, sums,
            pltpu.VMEM((rows, HEAD), jnp.bfloat16),
            pltpu.VMEM((8, HEAD), jnp.float32),
            block, sums, block, block,
        ] + [seven] * 10,
        compiler_params=pltpu.CompilerParams(collective_id=1, has_side_effects=True),
    )(log_decay, queries, key_rows, value_rows, gate_logits, norm_gain[None, :])


def project_kernel(
    a_ref, w_ref, sq_ref, o_ref,
    give, got, held, own, relay, landed, squares,
    give_send, give_recv, far_send, far_recv, near_send, near_recv,
    last_send, last_recv, sq_send, sq_recv,
):
    tokens, width = o_ref.shape
    half = tokens // 2
    tile = tokens // 3
    me = lax.axis_index("tp")
    core = lax.rem(me, 2)
    chip = lax.div(me, 2)

    def device(step, which):
        return lax.rem(chip + step, 4) * 2 + which

    sibling = device(0, 1 - core)
    right, left = device(1, core), device(3, core)

    barrier = pltpu.get_barrier_semaphore()
    for offset in range(1, 8):
        pl.semaphore_signal(
            barrier, inc=1, device_id={"tp": lax.rem(me + offset, 8)},
            device_id_type=pl.DeviceIdType.MESH,
        )
    pl.semaphore_wait(barrier, 7)

    def send(source, target, send_sem, recv_sem, to):
        copy = pltpu.make_async_remote_copy(
            src_ref=source, dst_ref=target, send_sem=send_sem, recv_sem=recv_sem,
            device_id={"tp": to}, device_id_type=pl.DeviceIdType.MESH,
        )
        copy.start()
        return copy

    copies = []
    sq_copies = [
        send(sq_ref, squares.at[i], sq_send.at[i], sq_recv.at[i], lax.rem(me + i + 1, 8))
        for i in range(7)
    ]

    def tiles(body):
        def step(i, carry):
            body(pl.ds(pl.multiple_of(i * tile, tile), tile))
            return carry

        lax.fori_loop(0, 3, step, 0)

    def product(dest, rows):
        columns = pl.ds(pl.multiple_of(dest * width, 128), width)
        return jnp.dot(a_ref[rows, :], w_ref[:, columns], preferred_element_type=jnp.float32)

    steps = (2, 1, 3, 0)
    gives = []

    def hand_over(k):
        def body(rows):
            give[k, rows, :] = product(device(steps[k], 1 - core), rows).astype(jnp.bfloat16)

        tiles(body)
        gives.append(send(give.at[k], got.at[k], give_send.at[k], give_recv.at[k], sibling))

    def gather(k, target, dtype):
        def first(rows):
            own[rows, :] = product(device(steps[k], core), rows)

        tiles(first)
        gives[k].wait_recv()

        def second(rows):
            total = own[rows, :] + got[k, rows, :].astype(jnp.float32)
            if dtype is None:
                own[rows, :] = total
            else:
                target[k, rows, :] = total.astype(dtype)

        tiles(second)

    top, bottom = pl.ds(0, half), pl.ds(half, half)
    hand_over(0)
    hand_over(1)
    gather(0, held, jnp.bfloat16)
    far_right = send(held.at[0, top], relay.at[0], far_send.at[0], far_recv.at[0], right)
    far_left = send(held.at[0, bottom], relay.at[1], far_send.at[1], far_recv.at[1], left)
    hand_over(2)
    gather(1, held, jnp.bfloat16)
    near_right = send(
        held.at[1, bottom], landed.at[0, bottom], near_send.at[0], near_recv.at[0], right
    )
    hand_over(3)
    gather(2, held, jnp.bfloat16)
    near_left = send(held.at[2, top], landed.at[1, top], near_send.at[1], near_recv.at[1], left)
    gather(3, None, None)

    def merge(k, start, slot):
        piece = half // 3

        def step(i, carry):
            rows = pl.ds(pl.multiple_of(start + i * piece, piece), piece)
            here = pl.ds(pl.multiple_of(i * piece, piece), piece)
            total = held[k, rows, :].astype(jnp.float32) + relay[slot, here, :].astype(jnp.float32)
            held[k, rows, :] = total.astype(jnp.bfloat16)
            return carry

        lax.fori_loop(0, 3, step, 0)

    far_right.wait_recv()
    merge(1, 0, 0)
    last_right = send(held.at[1, top], landed.at[0, top], last_send.at[0], last_recv.at[0], right)
    far_left.wait_recv()
    merge(2, half, 1)
    last_left = send(
        held.at[2, bottom], landed.at[1, bottom], last_send.at[1], last_recv.at[1], left
    )
    total = sq_ref[...]
    for i in range(7):
        sq_copies[i].wait_recv()
        total = total + squares[i]
    scale = lax.rsqrt(total / (HEADS * HEAD) + 1e-06)
    scale = jnp.transpose(jnp.broadcast_to(scale, (8, tokens)))[:, :1]
    near_right.wait_recv()
    near_left.wait_recv()
    last_right.wait_recv()
    last_left.wait_recv()
    for i in range(3):
        rows = slice(i * tile, (i + 1) * tile)
        summed = (
            own[rows, :]
            + landed[0, rows, :].astype(jnp.float32)
            + landed[1, rows, :].astype(jnp.float32)
        )
        o_ref[rows, :] = (summed * scale[rows]).astype(o_ref.dtype)
    for copy in sq_copies + gives + [
        far_right, far_left, near_right, near_left, last_right, last_left
    ]:
        copy.wait_send()


def project(attended, out_weight, squares):
    tokens = attended.shape[0]
    width = out_weight.shape[1] // 8
    block = (4, tokens, width)
    pair = pltpu.SemaphoreType.DMA((2,))
    four = pltpu.SemaphoreType.DMA((4,))
    seven = pltpu.SemaphoreType.DMA((7,))
    vmem = pl.BlockSpec(memory_space=pltpu.VMEM)
    return pl.pallas_call(
        project_kernel,
        out_shape=jax.ShapeDtypeStruct((tokens, width), jnp.bfloat16),
        in_specs=[vmem] * 3,
        out_specs=vmem,
        scratch_shapes=[
            pltpu.VMEM(block, jnp.bfloat16),
            pltpu.VMEM(block, jnp.bfloat16),
            pltpu.VMEM((3, tokens, width), jnp.bfloat16),
            pltpu.VMEM((tokens, width), jnp.float32),
            pltpu.VMEM((2, tokens // 2, width), jnp.bfloat16),
            pltpu.VMEM((2, tokens, width), jnp.bfloat16),
            pltpu.VMEM((7, 1, tokens), jnp.float32),
            four, four, pair, pair, pair, pair, pair, pair, seven, seven,
        ],
        compiler_params=pltpu.CompilerParams(
            collective_id=0, has_side_effects=True, vmem_limit_bytes=40 << 20
        ),
    )(attended, out_weight, squares)


def shards(queries, key_rows, value_rows, log_decay, gate_logits, norm_gain, out_weight):
    attended, squares = exchange(
        log_decay, queries, key_rows, value_rows, gate_logits, norm_gain
    )
    return project(attended, out_weight, squares)


def solution(mesh):
    return jax.shard_map(
        shards,
        mesh=mesh,
        in_specs=(
            P("seq", "tp"),
            P("seq", "tp"),
            P("seq", "tp"),
            P("tp", "seq"),
            P("seq", "tp"),
            P("tp"),
            P("tp", None),
        ),
        out_specs=P("seq", "tp"),
        check_vma=False,
    )
```
